32 devices in a mesh: dp: 32 (over z, y, x, core).
Axes of the slice: x: 2, y: 2, z: 4, core: 2. Of those that a mesh axis runs over, the one named last changes fastest.
Arguments:
- tokens: bfloat16 [192, 2, 197, 384], P('dp'), may hold values from -60 to 60
- counts: int32 [192], P('dp'), may hold values from 1 to 2, as said below
- cotangent: float32 [192, 2, 197, 384], P('dp'), may hold values from -6 to 6
- norm_gain: float32 [2, 2, 384], P(None, None, 'dp'), may hold values from 0.5 to 1.5
- bias_rows: float32 [2, 6, 384], P(None, None, 'dp'), may hold values from -1.8 to 1.8
- up_bias: float32 [2, 1536], P(None, 'dp'), may hold values from -1.8 to 1.8
- qkv_weight: float32 [2, 384, 1152], P(None, 'dp'), may hold values from -12 to 12
- out_weight: float32 [2, 384, 384], P(None, 'dp'), may hold values from -1.25 to 1.25
- up_weight: float32 [2, 384, 1536], P(None, 'dp'), may hold values from -0.3125 to 0.3125
- down_weight: float32 [2, 1536, 384], P(None, 'dp'), may hold values from -0.15625 to 0.15625
- first_norm_gain: float32 [2, 2, 384], P(None, None, 'dp'), may hold values from -0.06 to 0.06
- first_bias_rows: float32 [2, 6, 384], P(None, None, 'dp'), may hold values from -0.06 to 0.06
- first_up_bias: float32 [2, 1536], P(None, 'dp'), may hold values from -0.06 to 0.06
- first_qkv_weight: float32 [2, 384, 1152], P(None, 'dp'), may hold values from -0.06 to 0.06
- first_out_weight: float32 [2, 384, 384], P(None, 'dp'), may hold values from -0.06 to 0.06
- first_up_weight: float32 [2, 384, 1536], P(None, 'dp'), may hold values from -0.06 to 0.06
- first_down_weight: float32 [2, 1536, 384], P(None, 'dp'), may hold values from -0.06 to 0.06
- second_norm_gain: float32 [2, 2, 384], P(None, None, 'dp'), may hold values from 1e-05 to 0.001
- second_bias_rows: float32 [2, 6, 384], P(None, None, 'dp'), may hold values from 1e-05 to 0.001
- second_up_bias: float32 [2, 1536], P(None, 'dp'), may hold values from 1e-05 to 0.001
- second_qkv_weight: float32 [2, 384, 1152], P(None, 'dp'), may hold values from 1e-05 to 0.001
- second_out_weight: float32 [2, 384, 384], P(None, 'dp'), may hold values from 1e-05 to 0.001
- second_up_weight: float32 [2, 384, 1536], P(None, 'dp'), may hold values from 1e-05 to 0.001
- second_down_weight: float32 [2, 1536, 384], P(None, 'dp'), may hold values from 1e-05 to 0.001
Outputs:
- block_out: float32 [192, 2, 197, 384], P('dp')
- input_grad: float32 [192, 2, 197, 384], P('dp')
- grad_norm_gain: float32 [2, 2, 384], P(None, None, 'dp')
- grad_bias_rows: float32 [2, 6, 384], P(None, None, 'dp')
- grad_up_bias: float32 [2, 1536], P(None, 'dp')
- grad_qkv_weight: float32 [2, 384, 1152], P(None, 'dp')
- grad_out_weight: float32 [2, 384, 384], P(None, 'dp')
- grad_up_weight: float32 [2, 384, 1536], P(None, 'dp')
- grad_down_weight: float32 [2, 1536, 384], P(None, 'dp')
- new_norm_gain: float32 [2, 2, 384], P(None, None, 'dp')
- new_bias_rows: float32 [2, 6, 384], P(None, None, 'dp')
- new_up_bias: float32 [2, 1536], P(None, 'dp')
- new_qkv_weight: float32 [2, 384, 1152], P(None, 'dp')
- new_out_weight: float32 [2, 384, 384], P(None, 'dp')
- new_up_weight: float32 [2, 384, 1536], P(None, 'dp')
- new_down_weight: float32 [2, 1536, 384], P(None, 'dp')
- new_first_norm_gain: float32 [2, 2, 384], P(None, None, 'dp')
- new_first_bias_rows: float32 [2, 6, 384], P(None, None, 'dp')
- new_first_up_bias: float32 [2, 1536], P(None, 'dp')
- new_first_qkv_weight: float32 [2, 384, 1152], P(None, 'dp')
- new_first_out_weight: float32 [2, 384, 384], P(None, 'dp')
- new_first_up_weight: float32 [2, 384, 1536], P(None, 'dp')
- new_first_down_weight: float32 [2, 1536, 384], P(None, 'dp')
- new_second_norm_gain: float32 [2, 2, 384], P(None, None, 'dp')
- new_second_bias_rows: float32 [2, 6, 384], P(None, None, 'dp')
- new_second_up_bias: float32 [2, 1536], P(None, 'dp')
- new_second_qkv_weight: float32 [2, 384, 1152], P(None, 'dp')
- new_second_out_weight: float32 [2, 384, 384], P(None, 'dp')
- new_second_up_weight: float32 [2, 384, 1536], P(None, 'dp')
- new_second_down_weight: float32 [2, 1536, 384], P(None, 'dp')
The draws below stay inside these ranges and needn't reach their ends.
Inputs may be any that keep to these rules, and one draw needn't show every extreme that they name: counts[g] images fill group g: slot 0 always, slot 1 only when counts[g] is 2; every draw has groups of both kinds.
All inputs are finite; a program needn't handle non-finite values.
Results may differ from the reference program's by a relative error of at most 0.02.
The reference program's roundings to bfloat16 on the way count: a program that leaves them out, or rounds other values in their place, can miss the bound.
Values may be sent and summed in bfloat16 or wider, within the bound.
No kernel may reach another device: no remote copies, remote signals or barrier semaphores. Data moves between devices by JAX's collectives and lax.ppermute only.
A program may use at most 320 MiB of HBM per device.

```python
import math
import jax
import jax.numpy as jnp
from jax import lax

D = 384
HD = 64
FF = 1536
SEQ = 197
LAYERS = 2
STEP = 3
GROUPS_DEV = 6
GROUPS = 192
N_DP = 32


def draw_tokens(key, part):
    first_key, second_key = jax.random.split(jax.random.fold_in(key, 3), 2)
    scales = jnp.exp(jax.random.uniform(first_key, (GROUPS, 2, SEQ, 1), jnp.float32) * 2.302585092994046)
    fresh = jax.random.truncated_normal(second_key, -5.9, 5.9, (GROUPS, 2, SEQ, D), jnp.float32)
    values = fresh
    return (values * scales).astype(jnp.bfloat16)


def draw_counts(key, part):
    first_key, second_key, third_key = jax.random.split(jax.random.fold_in(key, 7), 3)
    values = jax.random.randint(first_key, (GROUPS,), 1, 3)
    first_pos = jax.random.randint(second_key, (), 0, GROUPS)
    other_pos = (first_pos + 1 + jax.random.randint(third_key, (), 0, GROUPS - 1)) % GROUPS
    places = jnp.arange(GROUPS)
    values = jnp.where(places == first_pos, 2, values)
    values = jnp.where(places == other_pos, 1, values)
    return values.astype(jnp.int32)


def draw_qkv_weight(key, part):
    first_key = jax.random.fold_in(jax.random.fold_in(key, 11), 0)
    std = D ** (-0.5)
    whole = jax.random.truncated_normal(first_key, -6.0, 6.0, (LAYERS, D, 3 * D), jnp.float32) * std
    return whole


def shard_levels(own_key, extent, cuts, low, largest):
    def one(axis_at, blocks):
        draws = jax.random.uniform(jax.random.fold_in(jax.random.fold_in(own_key, 6), axis_at), (blocks,), jnp.float32, low / len(cuts), largest / len(cuts))
        return jnp.repeat(jnp.exp(draws), extent[axis_at] // blocks).reshape((-1,) + (1,) * (len(extent) - axis_at - 1))

    level = one(*cuts[0])
    for cut in cuts[1:]:
        level = level * one(*cut)
    return level


def centred(stream_key, shape, deviation, reach, shards=(), kind=jnp.bfloat16):
    values = deviation * jax.random.normal(stream_key, shape, jnp.float32)
    if shards:
        values = values * shard_levels(stream_key, shape, shards, -0.22, 0.18)
    return jnp.clip(values, -reach, reach).astype(kind)


def setup_inputs(seed: int = 0) -> dict:
    seeds = jax.random.split(jax.random.key(seed), 25)
    tokens = draw_tokens(jax.random.fold_in(seeds[24], 71), 0)
    counts = draw_counts(jax.random.fold_in(seeds[24], 71), 0)
    cotangent = centred(seeds[2], (GROUPS, 2, SEQ, D), 1.0, 6.0, ((0, 32),), jnp.float32)
    norm_gain = jnp.clip(1.0 + 0.1 * jax.random.normal(seeds[3], (LAYERS, 2, D), jnp.float32), 0.5, 1.5)
    bias_rows = centred(seeds[4], (LAYERS, 6, D), 0.3, 1.8, ((2, 32),), jnp.float32)
    up_bias = centred(seeds[5], (LAYERS, FF), 0.3, 1.8, ((1, 32),), jnp.float32)
    qkv_weight = draw_qkv_weight(jax.random.fold_in(seeds[24], 71), 0)
    out_weight = centred(seeds[7], (LAYERS, D, D), (D // 16) ** -0.5, 1.25, ((1, 32),), jnp.float32)
    up_weight = centred(seeds[8], (LAYERS, D, FF), D ** -0.5, 0.3125, ((1, 32),), jnp.float32)
    down_weight = centred(seeds[9], (LAYERS, FF, D), FF ** -0.5, 0.15625, ((1, 32),), jnp.float32)
    first_norm_gain = centred(seeds[10], (LAYERS, 2, D), 0.01, 0.06, ((2, 32),), jnp.float32)
    first_bias_rows = centred(seeds[11], (LAYERS, 6, D), 0.01, 0.06, ((2, 32),), jnp.float32)
    first_up_bias = centred(seeds[12], (LAYERS, FF), 0.01, 0.06, ((1, 32),), jnp.float32)
    first_qkv_weight = centred(seeds[13], (LAYERS, D, 3 * D), 0.01, 0.06, ((1, 32),), jnp.float32)
    first_out_weight = centred(seeds[14], (LAYERS, D, D), 0.01, 0.06, ((1, 32),), jnp.float32)
    first_up_weight = centred(seeds[15], (LAYERS, D, FF), 0.01, 0.06, ((1, 32),), jnp.float32)
    first_down_weight = centred(seeds[16], (LAYERS, FF, D), 0.01, 0.06, ((1, 32),), jnp.float32)
    second_norm_gain = jnp.clip(jnp.exp(math.log(0.001) - 4.6051703 * jax.random.uniform(seeds[17], (LAYERS, 2, D), jnp.float32) ** shard_levels(seeds[17], (LAYERS, 2, D), ((2, 32),), -0.2, 0.2)), 9.999999747378752e-06, 0.001)
    second_bias_rows = jnp.clip(jnp.exp(math.log(0.001) - 4.6051703 * jax.random.uniform(seeds[18], (LAYERS, 6, D), jnp.float32) ** shard_levels(seeds[18], (LAYERS, 6, D), ((2, 32),), -0.2, 0.2)), 9.999999747378752e-06, 0.001)
    second_up_bias = jnp.clip(jnp.exp(math.log(0.001) - 4.6051703 * jax.random.uniform(seeds[19], (LAYERS, FF), jnp.float32) ** shard_levels(seeds[19], (LAYERS, FF), ((1, 32),), -0.2, 0.2)), 9.999999747378752e-06, 0.001)
    second_qkv_weight = jnp.clip(jnp.exp(math.log(0.001) - 4.6051703 * jax.random.uniform(seeds[20], (LAYERS, D, 3 * D), jnp.float32) ** shard_levels(seeds[20], (LAYERS, D, 3 * D), ((1, 32),), -0.2, 0.2)), 9.999999747378752e-06, 0.001)
    second_out_weight = jnp.clip(jnp.exp(math.log(0.001) - 4.6051703 * jax.random.uniform(seeds[21], (LAYERS, D, D), jnp.float32) ** shard_levels(seeds[21], (LAYERS, D, D), ((1, 32),), -0.2, 0.2)), 9.999999747378752e-06, 0.001)
    second_up_weight = jnp.clip(jnp.exp(math.log(0.001) - 4.6051703 * jax.random.uniform(seeds[22], (LAYERS, D, FF), jnp.float32) ** shard_levels(seeds[22], (LAYERS, D, FF), ((1, 32),), -0.2, 0.2)), 9.999999747378752e-06, 0.001)
    second_down_weight = jnp.clip(jnp.exp(math.log(0.001) - 4.6051703 * jax.random.uniform(seeds[23], (LAYERS, FF, D), jnp.float32) ** shard_levels(seeds[23], (LAYERS, FF, D), ((1, 32),), -0.2, 0.2)), 9.999999747378752e-06, 0.001)
    return dict(tokens=tokens, counts=counts, cotangent=cotangent, norm_gain=norm_gain, bias_rows=bias_rows, up_bias=up_bias, qkv_weight=qkv_weight, out_weight=out_weight, up_weight=up_weight, down_weight=down_weight, first_norm_gain=first_norm_gain, first_bias_rows=first_bias_rows, first_up_bias=first_up_bias, first_qkv_weight=first_qkv_weight, first_out_weight=first_out_weight, first_up_weight=first_up_weight, first_down_weight=first_down_weight, second_norm_gain=second_norm_gain, second_bias_rows=second_bias_rows, second_up_bias=second_up_bias, second_qkv_weight=second_qkv_weight, second_out_weight=second_out_weight, second_up_weight=second_up_weight, second_down_weight=second_down_weight)


BETA_ONE = 0.9
BETA_TWO = 0.95
LEARN_RATE = 0.02
DECAY = 0.05
ADAM_EPS = 1e-08
NORM_EPS = 1e-06

def mixed(form, left, right):
    return jnp.einsum(form, left.astype(jnp.float32), right.astype(jnp.float32))

def cross_rows(left, right):
    return lax.dot_general(left, right, (((0,), (0,)), ((), ())), preferred_element_type=jnp.float32)

def back_dot(left, weight):
    return lax.dot_general(left, weight, (((1,), (1,)), ((), ())), preferred_element_type=jnp.float32)

def normalize(rows, gain, shift):
    center = rows - lax.optimization_barrier(jnp.mean(rows, axis=-1, keepdims=True))
    rstd = lax.rsqrt(lax.optimization_barrier(jnp.mean(center * center, axis=-1, keepdims=True)) + NORM_EPS)
    normed = center * rstd
    return (normed * gain + shift, normed, rstd)

def norm_back(grad_in, gain, normed, rstd):
    scaled = grad_in * gain
    return rstd * (scaled - lax.optimization_barrier(jnp.mean(scaled, axis=-1, keepdims=True)) - normed * lax.optimization_barrier(jnp.mean(scaled * normed, axis=-1, keepdims=True)))

def gelu_value(pre_act):
    return 0.5 * pre_act * (1.0 + lax.erf(pre_act * 0.7071067811865476))

def gelu_slope(pre_act):
    return 0.5 * (1.0 + lax.erf(pre_act * 0.7071067811865476)) + pre_act * jnp.exp(-0.5 * pre_act * pre_act) * 0.3989422804014327

def forward_layer(resid, weights, images):
    gain_rows, shift_rows, up_shift, qkv_w, out_w, up_w, down_w = weights
    width = resid.shape[1]
    heads = width // HD
    scale = HD ** (-0.5)
    gains = gain_rows.astype(jnp.float32)
    shifts = shift_rows.astype(jnp.float32)
    first_f, normed_one, rstd_one = normalize(resid, gains[0], shifts[0])
    first_in = first_f.astype(jnp.bfloat16)
    proj = jnp.dot(first_in, qkv_w, preferred_element_type=jnp.float32)
    query = ((proj[:, :width] + shifts[1]) * scale).astype(jnp.bfloat16).reshape(images, SEQ, heads, HD)
    keys = proj[:, width:2 * width].astype(jnp.bfloat16).reshape(images, SEQ, heads, HD)
    values = (proj[:, 2 * width:] + shifts[2]).astype(jnp.bfloat16).reshape(images, SEQ, heads, HD)
    scores = mixed('nqhd,nkhd->nhqk', query, keys)
    top = lax.optimization_barrier(jnp.max(scores, axis=-1, keepdims=True))
    expo = jnp.exp(scores - top)
    total = lax.optimization_barrier(jnp.sum(expo, axis=-1, keepdims=True))
    logsum = top + jnp.log(total)
    probs = (expo / total).astype(jnp.bfloat16)
    context = mixed('nhqk,nkhd->nqhd', probs, values).reshape(-1, width).astype(jnp.bfloat16)
    hidden_res = resid + jnp.dot(context, out_w, preferred_element_type=jnp.float32) + shifts[3]
    second_f, normed_two, rstd_two = normalize(hidden_res, gains[1], shifts[4])
    second_in = second_f.astype(jnp.bfloat16)
    pre_act = jnp.dot(second_in, up_w, preferred_element_type=jnp.float32) + up_shift.astype(jnp.float32)
    activ = gelu_value(pre_act).astype(jnp.bfloat16)
    result = hidden_res + jnp.dot(activ, down_w, preferred_element_type=jnp.float32) + shifts[5]
    saved = (first_in, normed_one, rstd_one, query, keys, values, logsum, context, normed_two, rstd_two, second_in, pre_act, activ)
    return (result, saved)

def backward_layer(grad_out, weights, saved, images):
    gain_rows, shift_rows, up_shift, qkv_w, out_w, up_w, down_w = weights
    first_in, normed_one, rstd_one, query, keys, values, logsum, context, normed_two, rstd_two, second_in, pre_act, activ = saved
    width = grad_out.shape[1]
    scale = HD ** (-0.5)
    gains = gain_rows.astype(jnp.float32)
    grad_low = grad_out.astype(jnp.bfloat16)
    grad_down = cross_rows(activ, grad_low)
    shift_five = lax.optimization_barrier(jnp.sum(grad_out, axis=0))
    dpre = back_dot(grad_low, down_w) * gelu_slope(pre_act)
    dpre_low = dpre.astype(jnp.bfloat16)
    grad_up = cross_rows(second_in, dpre_low)
    grad_upshift = lax.optimization_barrier(jnp.sum(dpre, axis=0))
    dsecond = back_dot(dpre_low, up_w)
    gain_two = lax.optimization_barrier(jnp.sum(dsecond * normed_two, axis=0))
    shift_four = lax.optimization_barrier(jnp.sum(dsecond, axis=0))
    dres = grad_out + norm_back(dsecond, gains[1], normed_two, rstd_two)
    dres_low = dres.astype(jnp.bfloat16)
    grad_outw = cross_rows(context, dres_low)
    shift_three = lax.optimization_barrier(jnp.sum(dres, axis=0))
    dctx = back_dot(dres_low, out_w).astype(jnp.bfloat16).reshape(query.shape)
    scores = mixed('nqhd,nkhd->nhqk', query, keys)
    probs = jnp.exp(scores - logsum)
    probs_low = probs.astype(jnp.bfloat16)
    dvals = mixed('nhqk,nqhd->nkhd', probs_low, dctx).reshape(-1, width)
    dprobs = mixed('nqhd,nkhd->nhqk', dctx, values)
    inner = lax.optimization_barrier(jnp.sum(probs * dprobs, axis=-1, keepdims=True))
    dscore = (probs * (dprobs - inner)).astype(jnp.bfloat16)
    dquery = (mixed('nhqk,nkhd->nqhd', dscore, keys) * scale).reshape(-1, width)
    dkeys = mixed('nhqk,nqhd->nkhd', dscore, query).reshape(-1, width)
    shift_one = lax.optimization_barrier(jnp.sum(dquery, axis=0))
    shift_two = lax.optimization_barrier(jnp.sum(dvals, axis=0))
    dproj = jnp.concatenate([dquery, dkeys, dvals], axis=1).astype(jnp.bfloat16)
    grad_qkv = cross_rows(first_in, dproj)
    dfirst = back_dot(dproj, qkv_w)
    gain_one = lax.optimization_barrier(jnp.sum(dfirst * normed_one, axis=0))
    shift_zero = lax.optimization_barrier(jnp.sum(dfirst, axis=0))
    dinput = dres + norm_back(dfirst, gains[0], normed_one, rstd_one)
    grads = (jnp.stack([gain_one, gain_two]), jnp.stack([shift_zero, shift_one, shift_two, shift_three, shift_four, shift_five]), grad_upshift, grad_qkv, grad_outw, grad_up, grad_down)
    return (dinput, grads)

def adam_update(grad_sum, weight, first, second, count_rows, decay_on):
    grad = grad_sum / count_rows
    first_new = BETA_ONE * first + (1.0 - BETA_ONE) * grad
    second_new = BETA_TWO * second + (1.0 - BETA_TWO) * grad * grad
    fix_one = 1.0 - BETA_ONE ** STEP
    fix_two = 1.0 - BETA_TWO ** STEP
    direction = first_new / fix_one / (jnp.sqrt(second_new / fix_two) + ADAM_EPS)
    if decay_on:
        direction = direction + DECAY * weight
    return (grad, weight - LEARN_RATE * direction, first_new, second_new)

def reference(tokens, counts, cotangent, norm_gain, bias_rows, up_bias, qkv_weight, out_weight, up_weight, down_weight, first_norm_gain, first_bias_rows, first_up_bias, first_qkv_weight, first_out_weight, first_up_weight, first_down_weight, second_norm_gain, second_bias_rows, second_up_bias, second_qkv_weight, second_out_weight, second_up_weight, second_down_weight):
    params = (norm_gain, bias_rows, up_bias, qkv_weight, out_weight, up_weight, down_weight)
    firsts = (first_norm_gain, first_bias_rows, first_up_bias, first_qkv_weight, first_out_weight, first_up_weight, first_down_weight)
    seconds = (second_norm_gain, second_bias_rows, second_up_bias, second_qkv_weight, second_out_weight, second_up_weight, second_down_weight)
    rounded = tuple((p.astype(jnp.bfloat16) for p in params))
    layer_sets = [tuple((p[layer] for p in rounded)) for layer in range(LAYERS)]
    images = GROUPS_DEV * 2
    blocks_in = tokens.reshape(N_DP, GROUPS_DEV, 2, SEQ, D)
    blocks_cot = cotangent.reshape(N_DP, GROUPS_DEV, 2, SEQ, D)
    blocks_cnt = counts.reshape(N_DP, GROUPS_DEV)

    def block_step(carry, block):
        block_tok, block_cot, block_cnt = block
        live = jnp.stack([jnp.ones_like(block_cnt), (block_cnt == 2).astype(jnp.int32)], axis=1).astype(jnp.float32)
        live_rows = jnp.broadcast_to(live[:, :, None], (GROUPS_DEV, 2, SEQ)).reshape(-1, 1)
        resid = block_tok.astype(jnp.float32).reshape(-1, D)
        saved_all = []
        for layer in range(LAYERS):
            resid, saved = forward_layer(resid, layer_sets[layer], images)
            saved_all.append(saved)
        grad = block_cot.reshape(-1, D) * live_rows
        grads_all = [None] * LAYERS
        for layer in reversed(range(LAYERS)):
            grad, grads_all[layer] = backward_layer(grad, layer_sets[layer], saved_all[layer], images)
        carry = tuple((carry[i] + jnp.stack([grads_all[layer][i] for layer in range(LAYERS)]) for i in range(7)))
        return (carry, ((resid * live_rows).reshape(GROUPS_DEV, 2, SEQ, D), (grad * live_rows).reshape(GROUPS_DEV, 2, SEQ, D)))
    start = tuple((jnp.zeros(p.shape, jnp.float32) for p in params))
    sums, (outs, dins) = lax.scan(block_step, start, (blocks_in, blocks_cot, blocks_cnt))
    count_rows = float(N_DP * GROUPS_DEV * 2 * SEQ)
    results = [adam_update(sums[i], params[i], firsts[i], seconds[i], count_rows, i >= 3) for i in range(7)]
    block_out = outs.reshape(GROUPS, 2, SEQ, D)
    input_grad = dins.reshape(GROUPS, 2, SEQ, D)
    return (block_out, input_grad, results[0][0], results[1][0], results[2][0], results[3][0], results[4][0], results[5][0], results[6][0], results[0][1], results[1][1], results[2][1], results[3][1], results[4][1], results[5][1], results[6][1], results[0][2], results[1][2], results[2][2], results[3][2], results[4][2], results[5][2], results[6][2], results[0][3], results[1][3], results[2][3], results[3][3], results[4][3], results[5][3], results[6][3])
```

```python
import functools

import jax
import jax.numpy as jnp
import numpy as np
from jax import lax
from jax.experimental import pallas as pl
from jax.experimental.pallas import tpu as pltpu
from jax.sharding import PartitionSpec as P

HD = 64
STEP = 3
LANES = 128

BETA_ONE = 0.9
BETA_TWO = 0.95
LEARN_RATE = 0.02
DECAY = 0.05
ADAM_EPS = 1e-08
NORM_EPS = 1e-06

BF = jnp.bfloat16
F4 = jnp.float32
VMEM_LIMIT = 63 * 1024 * 1024


def dot_nn(a, b):
    return lax.dot_general(a, b, (((1,), (0,)), ((), ())), preferred_element_type=F4)


def dot_nt(a, b):
    return lax.dot_general(a, b, (((1,), (1,)), ((), ())), preferred_element_type=F4)


def dot_tn(a, b):
    return lax.dot_general(a, b, (((0,), (0,)), ((), ())), preferred_element_type=F4)


def col_sum(x):
    return jnp.sum(x, axis=0, keepdims=True)


def normalize(rows, gain, shift):
    center = rows - jnp.mean(rows, axis=-1, keepdims=True)
    rstd = lax.rsqrt(jnp.mean(center * center, axis=-1, keepdims=True) + NORM_EPS)
    normed = center * rstd
    return (normed * gain + shift, normed, rstd)


def norm_back(grad_in, gain, normed, rstd):
    scaled = grad_in * gain
    return rstd * (
        scaled
        - jnp.mean(scaled, axis=-1, keepdims=True)
        - normed * jnp.mean(scaled * normed, axis=-1, keepdims=True)
    )


class Sizes:
    def __init__(self, n, images, seq, width, hidden, layers):
        assert n & (n - 1) == 0 and width % n == 0 and hidden % n == 0
        self.n, self.images, self.seq = n, images, seq
        self.width, self.hidden, self.layers = width, hidden, layers
        self.heads = width // HD
        self.rows = -(-seq // 16) * 16
        self.bits = n.bit_length() - 1
        self.kr, self.kd, self.ku = width // n, hidden // n, hidden // n
        cb = width // LANES
        self.segs = []
        at = 0
        for name, blocks, rows in (
            ("q", 3 * cb, self.kr),
            ("o", cb, self.kr),
            ("u", hidden // LANES, self.kr),
            ("d", cb, self.kd),
        ):
            self.segs.append((name, blocks, rows, at))
            at += blocks * rows
        self.small = -(-at // 8) * 8
        self.pack = self.small + 8
        third = -(-self.pack // 24) * 8
        self.parts = [(0, third), (third, third), (2 * third, self.pack - 2 * third)]
        mid = [1 << b for b in range(self.bits - 2, 0, -1)]
        top = [1 << (self.bits - 1)]
        self.orders = []
        for i in range(3):
            turn = (i * len(mid)) // 3
            self.orders.append(top + mid[turn:] + mid[:turn] + [1])
        self.group = 1
        while self.group * self.kr % 16:
            self.group *= 2

    def place(self, part):
        order = self.orders[part]
        out = []
        for rel in range(self.n):
            out.append(sum(((rel // b) & 1) << s for s, b in enumerate(order)))
        return out


def spec_any():
    return pl.BlockSpec(memory_space=pl.ANY)


def lane_iota():
    return lax.broadcasted_iota(jnp.int32, (8, LANES), 1)


def pack_kernel(sz, gain, bias, upb, wq, wo, wu, wd, *refs):
    outs, st = refs[:-1], refs[-1]
    src = {"q": wq, "o": wo, "u": wu, "d": wd}
    st[...] = jnp.zeros_like(st)
    for layer in range(sz.layers):
        for name, blocks, rows, at in sz.segs:
            for c in range(blocks):
                st[at + c * rows : at + (c + 1) * rows, :] = src[name][
                    layer, :, c * LANES : (c + 1) * LANES
                ]
        s = sz.small
        st[s : s + 2, 0 : sz.kr] = gain[layer]
        st[s + 2 : s + 8, 0 : sz.kr] = bias[layer]
        st[s : s + 1, 64 : 64 + sz.ku] = upb[layer : layer + 1, :]
        for p, (first, count) in enumerate(sz.parts):
            outs[layer * 3 + p][...] = st[first : first + count, :].astype(BF)


def pack_params(sz, params):
    shapes = [
        jax.ShapeDtypeStruct((count, LANES), BF)
        for _ in range(sz.layers)
        for _, count in sz.parts
    ]
    flat = pl.pallas_call(
        functools.partial(pack_kernel, sz),
        out_shape=shapes,
        scratch_shapes=[pltpu.VMEM((sz.pack, LANES), F4)],
        name="pack",
    )(*params)
    return [flat[3 * i : 3 * i + 3] for i in range(sz.layers)]


def swap(x, bit, n):
    return lax.ppermute(x, "dp", [(i, i ^ bit) for i in range(n)])


def gather_parts(sz, parts):
    held = [p[None] for p in parts]
    for s in range(sz.bits - 1):
        got = [swap(h, sz.orders[i][s], sz.n) for i, h in enumerate(held)]
        held = [jnp.concatenate([h, g], axis=0) for h, g in zip(held, got)]
    got = [swap(h, sz.orders[i][-1], sz.n) for i, h in enumerate(held)]
    return [x for pair in zip(held, got) for x in pair]


def scatter_parts(sz, halves):
    pairs = [tuple(halves[2 * i : 2 * i + 2]) for i in range(3)]
    for s in range(sz.bits - 1, 0, -1):
        got = [swap(send, sz.orders[i][s], sz.n) for i, (_, send) in enumerate(pairs)]
        half = (1 << s) // 2
        pairs = [
            (keep[:half] + g[:half], keep[half:] + g[half:])
            for (keep, _), g in zip(pairs, got)
        ]
    got = [swap(send, sz.orders[i][0], sz.n) for i, (_, send) in enumerate(pairs)]
    return [x for (keep, _), g in zip(pairs, got) for x in (keep, g)]


def read_weights(sz, tab, halves, gbuf, w, st, st_w, sems):
    half = sz.n // 2
    copies = []
    for p, (first, count) in enumerate(sz.parts):
        for side in range(2):
            copy = pltpu.make_async_copy(
                halves[2 * p + side],
                gbuf.at[pl.ds(side * half, half), pl.ds(first, count), :],
                sems.at[2 * p + side],
            )
            copy.start()
            copies.append(copy)
    for copy in copies:
        copy.wait()
    lane = lane_iota()
    span = sz.group

    @pl.loop(0, sz.n // span)
    def _(grp):
        for j in range(span):
            d = grp * span + j
            for p, (first, count) in enumerate(sz.parts):
                st[first : first + count, :] = gbuf[
                    tab[p * sz.n + d], first : first + count, :
                ].astype(F4)
            slot = 0
            for name, blocks, rows, at in sz.segs:
                for c in range(blocks):
                    st_w[slot, j * rows : (j + 1) * rows, :] = st[
                        at + c * rows : at + (c + 1) * rows, :
                    ]
                    slot += 1
        slot = 0
        for name, blocks, rows, at in sz.segs:
            base = pl.multiple_of(grp * (span * rows), 16)
            for c in range(blocks):
                w[name][pl.ds(base, span * rows), c * LANES : (c + 1) * LANES] = st_w[
                    slot, 0 : span * rows, :
                ].astype(BF)
                slot += 1

    last = 2
    gains = [jnp.zeros((8, LANES), F4) for _ in range(sz.width // LANES)]
    ups = [jnp.zeros((8, LANES), F4) for _ in range(sz.hidden // LANES)]
    for d in range(sz.n):
        v = gbuf[tab[last * sz.n + d], sz.small : sz.small + 8, :].astype(F4)
        for tiles, width, src in ((gains, sz.kr, 0), (ups, sz.ku, 64)):
            dst = d * width
            moved = pltpu.roll(v, (dst - src) % LANES, 1)
            for t in range(dst // LANES, (dst + width - 1) // LANES + 1):
                lo, hi = dst - t * LANES, dst + width - t * LANES
                tiles[t] = jnp.where((lane >= lo) & (lane < hi), moved, tiles[t])
    for t, tile in enumerate(gains):
        w["g"][:, t * LANES : (t + 1) * LANES] = tile
    for t, tile in enumerate(ups):
        w["b"][:, t * LANES : (t + 1) * LANES] = tile


def write_grads(sz, tab, acc, obuf, outs, st, sems):
    span = sz.group

    @pl.loop(0, sz.n // span)
    def _(grp):
        for j in range(span):
            d = grp * span + j
            for name, blocks, rows, at in sz.segs:
                base = pl.multiple_of(grp * (span * rows), 16)
                for c in range(blocks):
                    st[at + c * rows : at + (c + 1) * rows, :] = acc[name][
                        pl.ds(base, span * rows), c * LANES : (c + 1) * LANES
                    ][j * rows : (j + 1) * rows, :]
            for p, (first, count) in enumerate(sz.parts):
                stop = min(first + count, sz.small)
                obuf[tab[p * sz.n + d], first:stop, :] = st[first:stop, :].astype(BF)

    lane = lane_iota()
    row = lax.broadcasted_iota(jnp.int32, (8, LANES), 0)
    for d in range(sz.n):
        out = jnp.zeros((8, LANES), F4)
        for name, width, src in (("g", sz.kr, 0), ("b", sz.ku, 64)):
            dst = d * width
            for t in range(dst // LANES, (dst + width - 1) // LANES + 1):
                lo = max(dst - t * LANES, 0) - (dst - t * LANES) + src
                hi = min(dst + width - t * LANES, LANES) - (dst - t * LANES) + src
                tile = acc[name][:, t * LANES : (t + 1) * LANES]
                moved = pltpu.roll(tile, (src - dst) % LANES, 1)
                here = (lane >= lo) & (lane < hi)
                if name == "b":
                    here = here & (row == 0)
                out = jnp.where(here, moved, out)
        obuf[tab[2 * sz.n + d], sz.small : sz.small + 8, :] = out.astype(BF)

    half = sz.n // 2
    copies = []
    for p, (first, count) in enumerate(sz.parts):
        for side in range(2):
            copy = pltpu.make_async_copy(
                obuf.at[pl.ds(side * half, half), pl.ds(first, count), :],
                outs[2 * p + side],
                sems.at[2 * p + side],
            )
            copy.start()
            copies.append(copy)
    for copy in copies:
        copy.wait()


def half_mask(h):
    lane = lax.broadcasted_iota(jnp.int32, (1, LANES), 1)
    low = lane < HD
    return low if h % 2 == 0 else jnp.logical_not(low)


def head_of(ref, h):
    pair = ref[:, (h // 2) * LANES : (h // 2 + 1) * LANES]
    return jnp.where(half_mask(h), pair, jnp.zeros_like(pair))


def pair_of(ref, h):
    return ref[:, (h // 2) * LANES : (h // 2 + 1) * LANES]


def forward_image(sz, x, w, s):
    D = sz.width
    scale = HD ** (-0.5)
    g = w["g"]
    a1f, xn1, r1 = normalize(x, g[0:1, :], g[2:3, :])
    a1 = a1f.astype(BF)
    s["xn1"][...] = xn1
    s["r1"][...] = r1
    s["a1"][...] = a1
    s["q"][...] = ((dot_nn(a1, w["q"][:, 0:D]) + g[3:4, :]) * scale).astype(BF)
    s["k"][...] = dot_nn(a1, w["q"][:, D : 2 * D]).astype(BF)
    v = dot_nn(a1, w["q"][:, 2 * D : 3 * D]) + g[4:5, :]
    s["v"][...] = v.astype(BF)
    s["vt"][...] = v.T.astype(BF)
    row = lax.broadcasted_iota(jnp.int32, (sz.rows, 1), 0)
    for h in range(sz.heads):
        sc = dot_nt(pair_of(s["k"], h), head_of(s["q"], h))
        sc = jnp.where(row < sz.seq, sc, -1e30)
        top = jnp.max(sc, axis=0, keepdims=True)
        expo = jnp.exp(sc - top)
        total = jnp.sum(expo, axis=0, keepdims=True)
        probs = expo * (1.0 / total)
        s["p"][h] = probs
        s["ct"][h * HD : (h + 1) * HD, :] = dot_nn(
            s["vt"][h * HD : (h + 1) * HD, :], probs.astype(BF)
        )
    ctx = s["ct"][...].T.astype(BF)
    s["ctx"][...] = ctx
    h_res = x + dot_nn(ctx, w["o"][...]) + g[5:6, :]
    a2f, xn2, r2 = normalize(h_res, g[1:2, :], g[6:7, :])
    a2 = a2f.astype(BF)
    s["xn2"][...] = xn2
    s["r2"][...] = r2
    s["a2"][...] = a2
    u = dot_nn(a2, w["u"][...]) + w["b"][0:1, :]
    one_erf = 0.5 * (1.0 + lax.erf(u * 0.7071067811865476))
    s["z"][...] = (u * one_erf).astype(BF)
    s["gp"][...] = one_erf + u * jnp.exp(-0.5 * u * u) * 0.3989422804014327
    return h_res + dot_nn(s["z"][...], w["d"][...]) + g[7:8, :]


def backward_image(sz, dy, w, s, acc, t):
    D = sz.width
    scale = HD ** (-0.5)
    g = w["g"]
    dyb = dy.astype(BF)
    acc["d"][...] += dot_tn(s["z"][...], dyb)
    acc["g"][7:8, :] += col_sum(dy)
    du = dot_nt(dyb, w["d"][...]) * s["gp"][...]
    acc["b"][0:1, :] += col_sum(du)
    t["dub"][...] = du.astype(BF)
    dub = t["dub"][...]
    acc["u"][...] += dot_tn(s["a2"][...], dub)
    da2 = dot_nt(dub, w["u"][...])
    xn2 = s["xn2"][...]
    acc["g"][1:2, :] += col_sum(da2 * xn2)
    acc["g"][6:7, :] += col_sum(da2)
    dh = dy + norm_back(da2, g[1:2, :], xn2, s["r2"][...])
    dhb = dh.astype(BF)
    acc["o"][...] += dot_tn(s["ctx"][...], dhb)
    acc["g"][5:6, :] += col_sum(dh)
    t["dc"][...] = dot_nt(dhb, w["o"][...]).astype(BF)
    t["kt"][...] = s["k"][...].astype(F4).T.astype(BF)
    for pair in range(sz.heads // 2):
        dv = dk = None
        for h in (2 * pair, 2 * pair + 1):
            dch, qh = head_of(t["dc"], h), head_of(s["q"], h)
            dp = dot_nt(pair_of(s["v"], h), dch)
            probs = s["p"][h]
            inner = jnp.sum(probs * dp, axis=0, keepdims=True)
            ds = (probs * (dp - inner)).astype(BF)
            dvh, dkh = dot_nn(probs.astype(BF), dch), dot_nn(ds, qh)
            dv = dvh if dv is None else dv + dvh
            dk = dkh if dk is None else dk + dkh
            t["qt"][h * HD : (h + 1) * HD, :] = dot_nn(t["kt"][h * HD : (h + 1) * HD, :], ds) * scale
        at = pair * LANES
        acc["g"][4:5, at : at + LANES] += col_sum(dv)
        t["dp"][:, D + at : D + at + LANES] = dk.astype(BF)
        t["dp"][:, 2 * D + at : 2 * D + at + LANES] = dv.astype(BF)
    dq = t["qt"][...].T
    acc["g"][3:4, :] += col_sum(dq)
    t["dp"][:, 0:D] = dq.astype(BF)
    dproj = t["dp"][...]
    acc["q"][...] += dot_tn(s["a1"][...], dproj)
    dfirst = dot_nt(dproj, w["q"][...])
    xn1 = s["xn1"][...]
    acc["g"][0:1, :] += col_sum(dfirst * xn1)
    acc["g"][2:3, :] += col_sum(dfirst)
    return dh + norm_back(dfirst, g[0:1, :], xn1, s["r1"][...])


WEIGHTS = ("q", "o", "u", "d", "g", "b")
SAVED = ("xn1", "r1", "a1", "q", "k", "v", "p", "ctx", "xn2", "r2", "a2", "z", "gp")
TEMPS = ("dub", "dc", "kt", "qt", "dp")


def weight_scratch(sz, kind):
    D, FF = sz.width, sz.hidden
    return [
        pltpu.VMEM((D, 3 * D), kind),
        pltpu.VMEM((D, D), kind),
        pltpu.VMEM((D, FF), kind),
        pltpu.VMEM((FF, D), kind),
        pltpu.VMEM((8, D), F4),
        pltpu.VMEM((8, FF), F4),
    ]


def load_scratch(sz):
    most = max(rows for _, _, rows, _ in sz.segs) * sz.group
    slots = sum(blocks for _, blocks, _, _ in sz.segs)
    return [
        pltpu.VMEM((sz.n, sz.pack, LANES), BF),
        pltpu.VMEM((sz.pack, LANES), F4),
        pltpu.VMEM((slots, most, LANES), F4),
        pltpu.SemaphoreType.DMA((6,)),
    ]


def saved_shapes(sz):
    R, D, FF = sz.rows, sz.width, sz.hidden
    return {
        "xn1": ((R, D), F4),
        "r1": ((R, 1), F4),
        "a1": ((R, D), BF),
        "q": ((R, D), BF),
        "k": ((R, D), BF),
        "v": ((R, D), BF),
        "p": ((sz.heads, R, R), F4),
        "ctx": ((R, D), BF),
        "xn2": ((R, D), F4),
        "r2": ((R, 1), F4),
        "a2": ((R, D), BF),
        "z": ((R, FF), BF),
        "gp": ((R, FF), F4),
    }


def local_shapes(sz):
    R, D, FF = sz.rows, sz.width, sz.hidden
    return {"vt": ((D, R), BF), "ct": ((D, R), F4)}


def temp_shapes(sz):
    R, D, FF = sz.rows, sz.width, sz.hidden
    return {
        "dub": ((R, FF), BF),
        "dc": ((R, D), BF),
        "kt": ((D, R), BF),
        "qt": ((D, R), F4),
        "dp": ((R, 3 * D), BF),
    }


def named(names, refs):
    return dict(zip(names, refs))


def first_kernel(sz, tab, tokens, *refs):
    refs = list(refs)
    take = lambda k: [refs.pop(0) for _ in range(k)]
    halves = take(6)
    (x1,) = take(1)
    saved = {k: r.at[0] for k, r in named(SAVED, take(len(SAVED))).items()}
    w = named(WEIGHTS, take(6))
    gbuf, st, st_w, sems = take(4)
    (xs,) = take(1)
    local = named(("vt", "ct"), take(2))
    i = pl.program_id(0)

    @pl.when(i == 0)
    def _():
        read_weights(sz, tab, halves, gbuf, w, st, st_w, sems)
        xs[...] = jnp.zeros_like(xs)

    @pl.when(tab[3 * sz.n + i] == 1)
    def _():
        xs[0 : sz.seq, :] = tokens[0].astype(F4)
        x1[0] = forward_image(sz, xs[...], w, {**saved, **local})


def second_kernel(sz, tab, x1, cot, *refs):
    refs = list(refs)
    take = lambda k: [refs.pop(0) for _ in range(k)]
    halves = take(6)
    out, dx = take(2)
    packed = take(6)
    w = named(WEIGHTS, take(6))
    acc = named(WEIGHTS, take(6))
    gbuf, st, st_w, sems = take(4)
    (dys,) = take(1)
    saved = named(SAVED, take(len(SAVED)))
    local = named(("vt", "ct"), take(2))
    temps = named(TEMPS, take(5))
    i = pl.program_id(0)

    @pl.when(i == 0)
    def _():
        read_weights(sz, tab, halves, gbuf, w, st, st_w, sems)
        for name in WEIGHTS:
            acc[name][...] = jnp.zeros_like(acc[name])
        dys[...] = jnp.zeros_like(dys)

    live = tab[3 * sz.n + i] == 1

    @pl.when(live)
    def _():
        s = {**saved, **local}
        y = forward_image(sz, x1[0], w, s)
        out[0] = y[0 : sz.seq, :]
        dys[0 : sz.seq, :] = cot[0]
        dx[0] = backward_image(sz, dys[...], w, s, acc, temps)

    @pl.when(jnp.logical_not(live))
    def _():
        out[0] = jnp.zeros(out.shape[1:], F4)

    @pl.when(i == sz.images - 1)
    def _():
        write_grads(sz, tab, acc, gbuf, packed, st, sems)


def third_kernel(sz, tab, dx, *refs):
    refs = list(refs)
    take = lambda k: [refs.pop(0) for _ in range(k)]
    saved = {k: r.at[0] for k, r in named(SAVED, take(len(SAVED))).items()}
    halves = take(6)
    (out,) = take(1)
    packed = take(6)
    w = named(WEIGHTS, take(6))
    acc = named(WEIGHTS, take(6))
    gbuf, st, st_w, sems = take(4)
    temps = named(TEMPS, take(5))
    i = pl.program_id(0)

    @pl.when(i == 0)
    def _():
        read_weights(sz, tab, halves, gbuf, w, st, st_w, sems)
        for name in WEIGHTS:
            acc[name][...] = jnp.zeros_like(acc[name])

    live = tab[3 * sz.n + i] == 1

    @pl.when(live)
    def _():
        out[0] = backward_image(sz, dx[0], w, saved, acc, temps)[0 : sz.seq, :]

    @pl.when(jnp.logical_not(live))
    def _():
        out[0] = jnp.zeros(out.shape[1:], F4)

    @pl.when(i == sz.images - 1)
    def _():
        write_grads(sz, tab, acc, gbuf, packed, st, sems)


def image_spec(shape):
    zeros = (0,) * len(shape)
    return pl.BlockSpec((1,) + tuple(shape), lambda i, tab: (i,) + zeros)


def scratch_of(shapes, names):
    return [pltpu.VMEM(*shapes[k]) for k in names]


def packed_outs(sz):
    return [
        jax.ShapeDtypeStruct((sz.n // 2, count, LANES), BF)
        for _, count in sz.parts
        for _ in range(2)
    ]


def params():
    return pltpu.CompilerParams(
        dimension_semantics=("arbitrary",), vmem_limit_bytes=VMEM_LIMIT
    )


def run_first(sz, tab, tokens, halves):
    saved = saved_shapes(sz)
    outs = [((sz.rows, sz.width), F4)] + [saved[k] for k in SAVED]
    res = pl.pallas_call(
        functools.partial(first_kernel, sz),
        grid_spec=pltpu.PrefetchScalarGridSpec(
            num_scalar_prefetch=1,
            grid=(sz.images,),
            in_specs=[image_spec(tokens.shape[1:])] + [spec_any()] * 6,
            out_specs=[image_spec(shape) for shape, _ in outs],
            scratch_shapes=weight_scratch(sz, BF)
            + load_scratch(sz)
            + [pltpu.VMEM((sz.rows, sz.width), F4)]
            + scratch_of(local_shapes(sz), ("vt", "ct")),
        ),
        out_shape=[jax.ShapeDtypeStruct((sz.images,) + tuple(a), b) for a, b in outs],
        compiler_params=params(),
        name="first",
    )(tab, tokens, *halves)
    return res[0], list(res[1:])


def run_second(sz, tab, x1, cot, halves):
    res = pl.pallas_call(
        functools.partial(second_kernel, sz),
        grid_spec=pltpu.PrefetchScalarGridSpec(
            num_scalar_prefetch=1,
            grid=(sz.images,),
            in_specs=[image_spec(x1.shape[1:]), image_spec(cot.shape[1:])] + [spec_any()] * 6,
            out_specs=[image_spec(cot.shape[1:]), image_spec(x1.shape[1:])] + [spec_any()] * 6,
            scratch_shapes=weight_scratch(sz, BF)
            + weight_scratch(sz, F4)
            + load_scratch(sz)
            + [pltpu.VMEM((sz.rows, sz.width), F4)]
            + scratch_of(saved_shapes(sz), SAVED)
            + scratch_of(local_shapes(sz), ("vt", "ct"))
            + scratch_of(temp_shapes(sz), TEMPS),
        ),
        out_shape=[
            jax.ShapeDtypeStruct(cot.shape, F4),
            jax.ShapeDtypeStruct(x1.shape, F4),
        ]
        + packed_outs(sz),
        compiler_params=params(),
        name="second",
    )(tab, x1, cot, *halves)
    return res[0], res[1], list(res[2:])


def run_third(sz, tab, dx, saved, halves):
    shape = (sz.images, sz.seq, sz.width)
    res = pl.pallas_call(
        functools.partial(third_kernel, sz),
        grid_spec=pltpu.PrefetchScalarGridSpec(
            num_scalar_prefetch=1,
            grid=(sz.images,),
            in_specs=[image_spec(dx.shape[1:])]
            + [image_spec(a.shape[1:]) for a in saved]
            + [spec_any()] * 6,
            out_specs=[image_spec(shape[1:])] + [spec_any()] * 6,
            scratch_shapes=weight_scratch(sz, BF)
            + weight_scratch(sz, F4)
            + load_scratch(sz)
            + scratch_of(temp_shapes(sz), TEMPS),
        ),
        out_shape=[jax.ShapeDtypeStruct(shape, F4)] + packed_outs(sz),
        compiler_params=params(),
        name="third",
    )(tab, dx, *saved, *halves)
    return res[0], list(res[1:])


def adam_math(grad_sum, weight, first, second, count_rows, decay_on):
    grad = grad_sum / count_rows
    first_new = BETA_ONE * first + (1.0 - BETA_ONE) * grad
    second_new = BETA_TWO * second + (1.0 - BETA_TWO) * grad * grad
    fix_one = 1.0 - BETA_ONE**STEP
    fix_two = 1.0 - BETA_TWO**STEP
    direction = first_new / fix_one / (jnp.sqrt(second_new / fix_two) + ADAM_EPS)
    if decay_on:
        direction = direction + DECAY * weight
    return (grad, weight - LEARN_RATE * direction, first_new, second_new)


def adam_kernel(sz, count_rows, *refs):
    refs = list(refs)
    take = lambda k: [refs.pop(0) for _ in range(k)]
    sums = [take(6) for _ in range(sz.layers)]
    state = [take(7) for _ in range(3)]
    outs = [take(7) for _ in range(4)]
    (st,) = take(1)

    def put(i, index, grad):
        vals = adam_math(grad, *(state[k][i][index] for k in range(3)), count_rows, i >= 3)
        for k in range(4):
            outs[k][i][index] = vals[k]

    for layer in range(sz.layers):
        for p, (first, count) in enumerate(sz.parts):
            a, b = sums[layer][2 * p : 2 * p + 2]
            st[first : first + count, :] = a[0].astype(F4) + b[0].astype(F4)
        s = sz.small
        put(0, layer, st[s : s + 2, 0 : sz.kr])
        put(1, layer, st[s + 2 : s + 8, 0 : sz.kr])
        put(2, (slice(layer, layer + 1), slice(None)), st[s : s + 1, 64 : 64 + sz.ku])
        for i, (name, blocks, rows, at) in enumerate(sz.segs):
            for c in range(blocks):
                index = (layer, slice(None), slice(c * LANES, (c + 1) * LANES))
                put(3 + i, index, st[at + c * rows : at + (c + 1) * rows, :])


def run_adam(sz, sums, params_, firsts, seconds, count_rows):
    shapes = [jax.ShapeDtypeStruct(p.shape, F4) for p in params_]
    res = pl.pallas_call(
        functools.partial(adam_kernel, sz, count_rows),
        out_shape=shapes * 4,
        scratch_shapes=[pltpu.VMEM((sz.pack, LANES), F4)],
        compiler_params=pltpu.CompilerParams(vmem_limit_bytes=VMEM_LIMIT),
        name="adam",
    )(*[x for layer in sums for x in layer], *params_, *firsts, *seconds)
    return res


def body(tokens, counts, cotangent, *state):
    params_, firsts, seconds = state[0:7], state[7:14], state[14:21]
    groups, _, seq, width = tokens.shape
    images = 2 * groups
    n = lax.axis_size("dp")
    layers, hidden = params_[3].shape[0], params_[5].shape[2]
    sz = Sizes(n, images, seq, width, hidden, layers)

    me = lax.axis_index("dp")
    table = []
    for p in range(3):
        place = np.asarray(sz.place(p), np.int32)
        mine = sum(((me >> (b.bit_length() - 1)) & 1) << s for s, b in enumerate(sz.orders[p]))
        table.append(jnp.bitwise_xor(jnp.asarray(place), mine.astype(jnp.int32)))
    live = jnp.stack([jnp.ones_like(counts), (counts == 2).astype(jnp.int32)], axis=1)
    tab = jnp.concatenate(table + [live.reshape(-1)])

    packed = pack_params(sz, params_)
    halves = [gather_parts(sz, packed[layer]) for layer in range(layers)]
    x1, saved = run_first(sz, tab, tokens.reshape(images, seq, width), halves[0])
    out, dx, grads_one = run_second(
        sz, tab, x1, cotangent.reshape(images, seq, width), halves[1]
    )
    sums_one = scatter_parts(sz, grads_one)
    input_grad, grads_zero = run_third(sz, tab, dx, saved, halves[0])
    sums_zero = scatter_parts(sz, grads_zero)
    res = run_adam(sz, [sums_zero, sums_one], params_, firsts, seconds, float(n * images * seq))
    return (out.reshape(tokens.shape), input_grad.reshape(tokens.shape), *res)


def solution(mesh):
    tok = P("dp", None, None, None)
    state = [P(None, None, "dp")] * 2 + [P(None, "dp")] + [P(None, "dp", None)] * 4
    return jax.shard_map(
        body,
        mesh=mesh,
        in_specs=(tok, P("dp"), tok, *(state * 3)),
        out_specs=(tok, tok, *(state * 4)),
        check_vma=False,
    )
```
